32 devices in a mesh: replica: 2 (over y), tp: 4 (over x, core), dp: 4 (over z).
Axes of the slice: x: 2, y: 2, z: 4, core: 2. Of those that a mesh axis runs over, the one named last changes fastest.
Arguments:
- tokens: bfloat16 [8192, 8192], P(('replica', 'dp'), 'tp'), parts along dimension 0, may hold values from -6 to 6
- query_weight: bfloat16 [8192, 4096], P(None, 'tp'), may hold values from -0.0625 to 0.0625
- value_weight: bfloat16 [8192, 1024], P(None, 'tp'), may hold values from -0.0625 to 0.0625
- adapter_down_factors: bfloat16 [256, 8192, 128], P('dp', 'tp'), may hold values from -0.0625 to 0.0625
- query_up_factors: bfloat16 [256, 64, 4096], P('dp', None, 'tp'), may hold values from -0.75 to 0.75
- value_up_factors: bfloat16 [256, 64, 1024], P('dp', None, 'tp'), may hold values from -0.75 to 0.75
- request_adapter: int32 [32], P('replica'), parts along dimension 0, may hold values from 0 to 255
- lengths: int32 [32], P('replica'), parts along dimension 0, may hold values from 1 to 1024, 4096 in all
- home: int32 [256], replicated, may hold values from 0 to 255, each once
Outputs:
- query: bfloat16 [8192, 4096], P(('replica', 'dp'), 'tp'), parts along dimension 0
- value: bfloat16 [8192, 1024], P(('replica', 'dp'), 'tp'), parts along dimension 0
The draws below stay inside these ranges and needn't reach their ends.
There are 2 independent parts, one for each index of `replica`. The reference program is written for one: setup_inputs(seed, part) draws one part's arguments, and reference() takes and returns one part's arrays. A program takes and returns all parts, laid end to end along the dimension named above; an argument that names none is the same for every part. Nothing has to cross between parts.
Inputs may be any that keep to these rules, and one draw needn't show every extreme that they name: The lengths sum to 4096; the requests lie one after another in the token order. `home`: each of 0 to 255 appears once.
All inputs are finite; a program needn't handle non-finite values.
Results may differ from the reference program's by a relative error of at most 0.0031.
Values may be sent and summed in bfloat16 or wider, within the bound.
A program may use at most 192 MiB of HBM per device.

```python
import math
import jax
import jax.numpy as jnp
import numpy as np
from jax import lax

MODEL_WIDTH = 8192
QUERY_FEATURES = 4096
VALUE_FEATURES = 1024
ADAPTER_RANK = 64
ADAPTER_STORE = 256
REPLICA_REQUESTS = 16
TOKENS = 4096
LONGEST = 1024


def plant(result, key, least, top_value):
    index_at = [jax.random.randint(jax.random.fold_in(key, axis), (), 0, length) for axis, length in enumerate(result.shape)]
    longest = result.shape.index(max(result.shape))
    next_to = index_at[:longest] + [(index_at[longest] + 1) % result.shape[longest]] + index_at[longest + 1:]
    return result.at[tuple(index_at)].set(least).at[tuple(next_to)].set(top_value)


def levels(key, extent, cuts, low, largest):
    def one(axis_at, blocks):
        draws = jax.random.uniform(jax.random.fold_in(jax.random.fold_in(key, 6), axis_at), (blocks,), jnp.float32, low / len(cuts), largest / len(cuts))
        return jnp.repeat(jnp.exp(draws), extent[axis_at] // blocks).reshape((-1,) + (1,) * (len(extent) - axis_at - 1))

    level = one(*cuts[0])
    for cut in cuts[1:]:
        level = level * one(*cut)
    return level


def cumulative_ranks(amount, slope):
    weights = [(1 << 20) // math.isqrt(standing ** slope) + 1 for standing in range(1, amount + 1)]
    width = 1 + sum(weights) // (1 << 30)
    return np.cumsum(np.array([max(1, weight // width) for weight in weights]))


def ranked_ids(key, extent, number_of, lean):
    grid = cumulative_ranks(number_of, lean)
    lot = jax.random.randint(jax.random.fold_in(key, 1), extent, 0, int(grid[number_of - 1]))
    rank = jnp.searchsorted(jnp.asarray(grid, jnp.int32), lot, side="right")
    return jax.random.permutation(jax.random.fold_in(key, 2), number_of)[rank].astype(jnp.int32)


def split_up(count, total, most, lean):
    portions = [(1 << 20) // math.isqrt(rank ** lean) + 1 for rank in range(2, count + 1)]
    rest, holding = total - most - (count - 1), [1] * (count - 1)
    while rest > 0:
        candidates = [i for i in range(count - 1) if holding[i] < most]
        whole, remaining = sum([portions[i] for i in candidates]), rest
        for i in candidates:
            more = min(most - holding[i], max(1, remaining * portions[i] // whole), rest)
            holding[i] = holding[i] + more
            rest = rest - more
    return np.array([most] + holding)


def ragged(rng, number_of, total, most, slope):
    if number_of == 2:
        one = jax.random.randint(rng, (), max(1, total - most), min(most, total - 1) + 1)
        return jnp.stack([one, total - one])
    sizes = jnp.asarray(split_up(number_of, total, most, slope), jnp.int32)
    pairs = (number_of - 1) // 2
    giver, receiver = sizes[1:1 + 2 * pairs:2], sizes[2:2 + 2 * pairs:2]
    room = jnp.minimum(giver - 1, most - receiver)
    moved = jax.random.randint(jax.random.fold_in(rng, 1), (pairs,), 0, 1 << 20) % (room + 1)
    sizes = sizes.at[1:1 + 2 * pairs:2].set(giver - moved).at[2:2 + 2 * pairs:2].set(receiver + moved)
    return sizes[jax.random.permutation(jax.random.fold_in(rng, 2), number_of)]


def noise(key, dims, deviation, reach, pieces=(), held_as=jnp.bfloat16):
    result = jax.random.normal(key, dims, jnp.float32) * deviation
    if len(pieces) > 0:
        result = levels(key, dims, pieces, -0.22, 0.18) * result
    return jnp.clip(result, min=-reach, max=reach).astype(held_as)


def setup_inputs(seed: int = 0, part: int = 0) -> dict:
    arg_keys = jax.random.split(jax.random.key(seed), 10)
    part_splits = jax.random.split(jax.random.fold_in(arg_keys[9], part), 10)
    return {
        "tokens": noise(part_splits[0], (TOKENS, MODEL_WIDTH), 1.0, 6.0, ((0, 4), (1, 4))),
        "query_weight": noise(arg_keys[1], (MODEL_WIDTH, QUERY_FEATURES), MODEL_WIDTH ** -0.5, 0.0625, ((1, 4),)),
        "value_weight": noise(arg_keys[2], (MODEL_WIDTH, VALUE_FEATURES), MODEL_WIDTH ** -0.5, 0.0625, ((1, 4),)),
        "adapter_down_factors": noise(arg_keys[3], (ADAPTER_STORE, MODEL_WIDTH, 2 * ADAPTER_RANK), MODEL_WIDTH ** -0.5, 0.0625, ((0, 4), (1, 4))),
        "query_up_factors": noise(arg_keys[4], (ADAPTER_STORE, ADAPTER_RANK, QUERY_FEATURES), ADAPTER_RANK ** -0.5, 0.75, ((0, 4), (2, 4))),
        "value_up_factors": noise(arg_keys[5], (ADAPTER_STORE, ADAPTER_RANK, VALUE_FEATURES), ADAPTER_RANK ** -0.5, 0.75, ((0, 4), (2, 4))),
        "request_adapter": plant(ranked_ids(part_splits[6], (REPLICA_REQUESTS,), ADAPTER_STORE, 2), jax.random.fold_in(part_splits[6], 3), 0, ADAPTER_STORE - 1).astype(jnp.int32),
        "lengths": ragged(part_splits[7], REPLICA_REQUESTS, TOKENS, LONGEST, 2).astype(jnp.int32),
        "home": jax.random.permutation(arg_keys[8], ADAPTER_STORE).astype(jnp.int32),
    }


adapter_scale = 0.5


def reference(tokens, query_weight, value_weight, adapter_down_factors, query_up_factors, value_up_factors, request_adapter, lengths, home):
    starts = jnp.cumsum(lengths, dtype=jnp.int32) - lengths
    rows_all = jnp.arange(TOKENS, dtype=jnp.int32)
    owner = jnp.sum((rows_all[:, None] >= starts[None, :]).astype(jnp.int32), axis=1, dtype=jnp.int32) - 1
    inside = (rows_all - starts[owner]).astype(jnp.int32)
    adapter_slots = home[request_adapter]
    padded = jnp.concatenate([tokens, jnp.zeros((LONGEST, MODEL_WIDTH), tokens.dtype)], axis=0)

    def per_request(request_number):
        block_input = lax.dynamic_slice_in_dim(padded, starts[request_number].astype(jnp.int32), LONGEST, 0)
        return jnp.dot(block_input, adapter_down_factors[adapter_slots[request_number]], preferred_element_type=jnp.float32)

    blocks = lax.map(per_request, jnp.arange(REPLICA_REQUESTS, dtype=jnp.int32))
    down = blocks[owner, inside].astype(jnp.bfloat16)
    onehot = (owner[:, None] == jnp.arange(REPLICA_REQUESTS, dtype=jnp.int32)[None, :]).astype(down.dtype)
    expand_q = (onehot[:, :, None] * down[:, None, :ADAPTER_RANK]).reshape(TOKENS, REPLICA_REQUESTS * ADAPTER_RANK)
    expand_v = (onehot[:, :, None] * down[:, None, ADAPTER_RANK:]).reshape(TOKENS, REPLICA_REQUESTS * ADAPTER_RANK)
    query_stacked = query_up_factors[adapter_slots].reshape(REPLICA_REQUESTS * ADAPTER_RANK, QUERY_FEATURES)
    value_stacked = value_up_factors[adapter_slots].reshape(REPLICA_REQUESTS * ADAPTER_RANK, VALUE_FEATURES)
    query_plain = jnp.dot(tokens, query_weight, preferred_element_type=jnp.float32)
    value_plain = jnp.dot(tokens, value_weight, preferred_element_type=jnp.float32)
    query_lowrank = jnp.dot(expand_q, query_stacked, preferred_element_type=jnp.float32)
    value_lowrank = jnp.dot(expand_v, value_stacked, preferred_element_type=jnp.float32)
    query = (query_plain + adapter_scale * query_lowrank).astype(jnp.bfloat16)
    value = (value_plain + adapter_scale * value_lowrank).astype(jnp.bfloat16)
    return (query, value)
```

```python
import functools

import jax
import jax.numpy as jnp
from jax import lax
from jax.experimental import pallas as pl
from jax.experimental.pallas import tpu as pltpu
from jax.sharding import PartitionSpec as P

adapter_scale = 0.5
LANES = 128
PARTS = 4
LAG = 3
ROWS = 128
MESH = pl.DeviceIdType.MESH
HBM = pl.BlockSpec(memory_space=pl.ANY)
SMEM = pl.BlockSpec(memory_space=pltpu.SMEM)
VMEM = pl.BlockSpec(memory_space=pltpu.VMEM)
GRANT = 60 << 20


def chunks_of(columns):
    return -(-columns // LANES)


def pack_kernel(keys, down_ref, up_q_ref, up_v_ref, out_ref):
    depth = down_ref.shape[1]
    rank = up_q_ref.shape[1]
    out_ref[0, pl.ds(0, depth), :] = down_ref[0]
    at = depth
    for ref in (up_q_ref, up_v_ref):
        columns = ref.shape[2]
        for j in range(chunks_of(columns)):
            width = min(LANES, columns - j * LANES)
            out_ref[0, pl.ds(at, rank), pl.ds(0, width)] = ref[0, :, pl.ds(j * LANES, width)]
            if width < LANES:
                out_ref[0, pl.ds(at, rank), pl.ds(width, LANES - width)] = jnp.zeros(
                    (rank, LANES - width), out_ref.dtype
                )
            at += rank


def pack(locations, down_f, up_q, up_v):
    count = locations.shape[0]
    depth, rank = down_f.shape[1], up_q.shape[1]
    height = depth + rank * (chunks_of(up_q.shape[2]) + chunks_of(up_v.shape[2]))
    return pl.pallas_call(
        pack_kernel,
        grid_spec=pltpu.PrefetchScalarGridSpec(
            num_scalar_prefetch=1,
            grid=(count,),
            in_specs=[
                pl.BlockSpec((1,) + t.shape[1:], lambda i, keys: (keys[i], 0, 0))
                for t in (down_f, up_q, up_v)
            ],
            out_specs=pl.BlockSpec((1, height, LANES), lambda i, keys: (i, 0, 0)),
        ),
        out_shape=jax.ShapeDtypeStruct((count, height, LANES), down_f.dtype),
        name="pack",
    )(locations, down_f, up_q, up_v)


def sweep_kernel(n, slots, spread, own_flag, packed, out, own, held, load_sem, send_sem, recv_sem, save_sem):
    me = lax.axis_index("dp")
    piece = held.shape[1] // PARTS
    steps = slots * PARTS
    barrier = pltpu.get_barrier_semaphore()
    has_low, has_high = me > 0, me < n - 1

    @pl.when(has_low)
    def _():
        pl.semaphore_signal(barrier, inc=1, device_id={"dp": me - 1}, device_id_type=MESH)

    @pl.when(has_high)
    def _():
        pl.semaphore_signal(barrier, inc=1, device_id={"dp": me + 1}, device_id_type=MESH)

    def load(i):
        return pltpu.make_async_copy(packed.at[i], own.at[i], load_sem.at[i])

    def start_load(i, carry):
        load(i).start()
        return carry

    lax.fori_loop(0, 2 * slots, start_load, 0)

    pl.semaphore_wait(barrier, has_low.astype(jnp.int32) + has_high.astype(jnp.int32))

    lower = me < n // 2

    def span(c):
        return lax.rem(c, PARTS) * piece

    def copy(stream, c, source, target):
        i = stream * slots + c // PARTS
        rows = pl.ds(span(c), piece)
        k = stream * steps + c
        return pltpu.make_async_remote_copy(
            src_ref=source.at[i, rows],
            dst_ref=held.at[i, rows],
            send_sem=send_sem.at[k],
            recv_sem=recv_sem.at[k],
            device_id={"dp": target},
            device_id_type=MESH,
        )

    def save(stream, c):
        i = stream * slots + c // PARTS
        rows = pl.ds(span(c), piece)
        return pltpu.make_async_copy(
            held.at[i, rows], out.at[stream * spread + c // PARTS, rows], save_sem.at[stream * steps + c]
        )

    def wait_load(i, carry):
        load(i).wait()
        return carry

    lax.fori_loop(0, 2 * slots, wait_load, 0)

    def first_sends(stream, target):
        def step(c, carry):
            copy(stream, c, own, target).start()
            return carry

        lax.fori_loop(0, steps, step, 0)

    @pl.when(jnp.logical_not(has_low))
    def _():
        first_sends(0, me + 1)

    @pl.when(jnp.logical_not(has_high))
    def _():
        first_sends(1, me - 1)

    def handle(stream, c):
        comes = has_low if stream == 0 else has_high
        goes = has_high if stream == 0 else has_low
        target = jnp.minimum(me + 1, n - 1) if stream == 0 else jnp.maximum(me - 1, 0)

        @pl.when(comes)
        def _():
            copy(stream, c, held, target).wait_recv()
            i = stream * slots + c // PARTS
            rows = pl.ds(pl.multiple_of(span(c), 16), piece)
            flag = own_flag[stream * spread + c // PARTS]
            held[i, rows, :] = jnp.where(flag > 0, own[i, rows, :], held[i, rows, :])

            @pl.when(goes)
            def _():
                copy(stream, c, held, target).start()

            save(stream, c).start()

    def step(t, carry):
        late = t - LAG

        @pl.when(jnp.logical_and(lower, t < steps))
        def _():
            handle(0, t)

        @pl.when(jnp.logical_and(lower, late >= 0))
        def _():
            handle(1, late)

        @pl.when(jnp.logical_and(jnp.logical_not(lower), t < steps))
        def _():
            handle(1, t)

        @pl.when(jnp.logical_and(jnp.logical_not(lower), late >= 0))
        def _():
            handle(0, late)

        return carry

    lax.fori_loop(0, steps + LAG, step, 0)

    def finish(c, carry):
        @pl.when(has_high)
        def _():
            copy(0, c, held, jnp.minimum(me + 1, n - 1)).wait_send()

        @pl.when(has_low)
        def _():
            copy(1, c, held, jnp.maximum(me - 1, 0)).wait_send()
            save(0, c).wait()

        @pl.when(has_high)
        def _():
            save(1, c).wait()

        return carry

    lax.fori_loop(0, steps, finish, 0)


def sweep(n, slots, spread, number, own_flag, packed):
    height = packed.shape[1]
    steps = slots * PARTS
    return pl.pallas_call(
        functools.partial(sweep_kernel, n, slots, spread),
        out_shape=jax.ShapeDtypeStruct((2 * spread, height, LANES), packed.dtype),
        in_specs=[SMEM, HBM],
        out_specs=HBM,
        scratch_shapes=[
            pltpu.VMEM((2 * slots, height, LANES), packed.dtype),
            pltpu.VMEM((2 * slots, height, LANES), packed.dtype),
            pltpu.SemaphoreType.DMA((2 * slots,)),
            pltpu.SemaphoreType.DMA((2 * steps,)),
            pltpu.SemaphoreType.DMA((2 * steps,)),
            pltpu.SemaphoreType.DMA((2 * steps,)),
        ],
        compiler_params=pltpu.CompilerParams(
            collective_id=number, has_side_effects=True, vmem_limit_bytes=GRANT
        ),
        name="sweep%d" % slots,
    )(own_flag, packed)


def down_kernel(first, last, low, high, source, place, tokens, swept, store, out, factor, sem):
    depth = factor.shape[1]

    def fetch(r, act):
        slot = lax.rem(r, 2)

        @pl.when(source[r] == 0)
        def _():
            act(pltpu.make_async_copy(store.at[place[r]], factor.at[slot], sem.at[slot]))

        @pl.when(source[r] != 0)
        def _():
            act(pltpu.make_async_copy(swept.at[place[r], pl.ds(0, depth)], factor.at[slot], sem.at[slot]))

    fetch(first[0], lambda c: c.start())

    def request(r, carry):
        @pl.when(r + 1 < last[0])
        def _():
            fetch(r + 1, lambda c: c.start())

        fetch(r, lambda c: c.wait())
        slot = lax.rem(r, 2)

        def block(k, inner):
            rows = pl.ds(pl.multiple_of(k * ROWS, ROWS), ROWS)
            product = jnp.dot(tokens[rows, :], factor[slot], preferred_element_type=jnp.float32)
            at = k * ROWS + lax.broadcasted_iota(jnp.int32, product.shape, 0)
            inside = jnp.logical_and(at >= low[r], at < high[r])
            out[rows, :] = jnp.where(inside, product, out[rows, :])
            return inner

        lax.fori_loop(low[r] // ROWS, (high[r] + ROWS - 1) // ROWS, block, 0)
        return carry

    lax.fori_loop(first[0], last[0], request, 0)


def down_products(scalars, tokens, swept, store):
    return pl.pallas_call(
        down_kernel,
        out_shape=jax.ShapeDtypeStruct((tokens.shape[0], store.shape[2]), jnp.float32),
        in_specs=[SMEM] * 6 + [VMEM, HBM, HBM],
        out_specs=VMEM,
        scratch_shapes=[
            pltpu.VMEM((2,) + store.shape[1:], store.dtype),
            pltpu.SemaphoreType.DMA((2,)),
        ],
        compiler_params=pltpu.CompilerParams(vmem_limit_bytes=24 << 20),
        name="down",
    )(*scalars, tokens, swept, store)


def up_kernel(
    first, last, low, high, source, place, down, base_q, base_v, swept, up_q, up_v,
    out_q, out_v, low_q, low_v, strip, own_q, own_v, sem,
):
    rank = own_q.shape[1]
    depth = swept.shape[1] - strip.shape[1]

    def fetch(r, act):
        slot = lax.rem(r, 2)

        @pl.when(source[r] == 0)
        def _():
            act(pltpu.make_async_copy(up_q.at[place[r]], own_q.at[slot], sem.at[slot, 0]))
            act(pltpu.make_async_copy(up_v.at[place[r]], own_v.at[slot], sem.at[slot, 1]))

        @pl.when(source[r] != 0)
        def _():
            act(pltpu.make_async_copy(
                swept.at[place[r], pl.ds(depth, strip.shape[1])], strip.at[slot], sem.at[slot, 0]))

    fetch(first[0], lambda c: c.start())

    def request(r, carry):
        @pl.when(r + 1 < last[0])
        def _():
            fetch(r + 1, lambda c: c.start())

        fetch(r, lambda c: c.wait())
        slot = lax.rem(r, 2)

        @pl.when(source[r] != 0)
        def _():
            at = 0
            for ref in (own_q, own_v):
                columns = ref.shape[2]
                for j in range(chunks_of(columns)):
                    width = min(LANES, columns - j * LANES)
                    ref[slot, :, pl.ds(j * LANES, width)] = strip[slot, pl.ds(at, rank), pl.ds(0, width)]
                    at += rank

        def block(k, inner):
            rows = pl.ds(pl.multiple_of(k * ROWS, ROWS), ROWS)
            at = k * ROWS + lax.broadcasted_iota(jnp.int32, (ROWS, 1), 0)
            inside = jnp.logical_and(at >= low[r], at < high[r])
            half = down[rows, :]
            for mine, factor, total in ((half[:, :rank], own_q, low_q), (half[:, rank:], own_v, low_v)):
                product = jnp.dot(mine, factor[slot], preferred_element_type=jnp.float32)
                total[rows, :] = jnp.where(inside, product, total[rows, :])
            return inner

        lax.fori_loop(low[r] // ROWS, (high[r] + ROWS - 1) // ROWS, block, 0)
        return carry

    lax.fori_loop(first[0], last[0], request, 0)

    def close(k, carry):
        rows = pl.ds(pl.multiple_of(k * ROWS, ROWS), ROWS)
        out_q[rows, :] = (base_q[rows, :] + adapter_scale * low_q[rows, :]).astype(out_q.dtype)
        out_v[rows, :] = (base_v[rows, :] + adapter_scale * low_v[rows, :]).astype(out_v.dtype)
        return carry

    lax.fori_loop(0, down.shape[0] // ROWS, close, 0)


def up_products(scalars, down, base_q, base_v, swept, up_q, up_v):
    strip = up_q.shape[1] * (chunks_of(up_q.shape[2]) + chunks_of(up_v.shape[2]))
    return pl.pallas_call(
        up_kernel,
        out_shape=[jax.ShapeDtypeStruct(b.shape, jnp.bfloat16) for b in (base_q, base_v)],
        in_specs=[SMEM] * 6 + [VMEM] * 3 + [HBM] * 3,
        out_specs=[VMEM, VMEM],
        scratch_shapes=[
            pltpu.VMEM(base_q.shape, jnp.float32),
            pltpu.VMEM(base_v.shape, jnp.float32),
            pltpu.VMEM((2, strip, LANES), swept.dtype),
            pltpu.VMEM((2,) + up_q.shape[1:], up_q.dtype),
            pltpu.VMEM((2,) + up_v.shape[1:], up_v.dtype),
            pltpu.SemaphoreType.DMA((2, 2)),
        ],
        compiler_params=pltpu.CompilerParams(vmem_limit_bytes=40 << 20),
        name="up",
    )(*scalars, down, base_q, base_v, swept, up_q, up_v)


def travel(goes, slot, holder, location):
    count = goes.shape[0]
    index = jnp.arange(count, dtype=jnp.int32)
    same = (slot[:, None] == slot[None, :]) & goes[None, :]
    first = jnp.min(jnp.where(same, index[None, :], count), axis=1)
    leads = goes & (first == index)
    position = jnp.sum((leads[None, :] & (index[None, :] < first[:, None])).astype(jnp.int32), axis=1)
    chosen = (leads[None, :] & (position[None, :] == index[:, None])).astype(jnp.int32)
    list_location = jnp.sum(chosen * location[None, :], axis=1)
    list_holder = jnp.sum(chosen * (holder[None, :] + 1), axis=1) - 1
    return position, list_location, list_holder, jnp.sum(leads.astype(jnp.int32))


def body(replicas, n, tokens, query_weight, value_weight, down_f, up_q, up_v, request_adapter, lengths, home):
    tok_rows = tokens.shape[0]
    stored = down_f.shape[0]
    count = request_adapter.shape[0]
    me = lax.axis_index("dp")
    index = jnp.arange(count, dtype=jnp.int32)
    wide = jnp.arange(home.shape[0], dtype=jnp.int32)
    slot = jnp.sum(jnp.where(request_adapter[:, None] == wide[None, :], home[None, :], 0), axis=1)
    starts = jnp.sum(jnp.where(index[None, :] < index[:, None], lengths[None, :], 0), axis=1)
    ends = starts + lengths
    holder, location = slot // stored, slot % stored
    begin, end = starts // tok_rows, (ends - 1) // tok_rows
    up_at, up_location, up_holder, up_count = travel(end > holder, slot, holder, location)
    dn_at, dn_location, dn_holder, dn_count = travel(begin < holder, slot, holder, location)
    need = jnp.maximum(up_count, dn_count).reshape(1)
    most = need
    for shift in range(1, replicas):
        other = lax.ppermute(need, "replica", [(i, (i + shift) % replicas) for i in range(replicas)])
        most = jnp.maximum(most, other)
    flags = jnp.concatenate([up_holder == me, dn_holder == me]).astype(jnp.int32)

    offset = me * tok_rows
    here = (begin <= me) & (end >= me)
    first = jnp.min(jnp.where(here, index, count)).reshape(1)
    last = jnp.max(jnp.where(here, index, -1)).reshape(1) + 1
    low = jnp.clip(starts - offset, 0, tok_rows)
    high = jnp.clip(ends - offset, 0, tok_rows)
    source = (holder != me).astype(jnp.int32)
    place = jnp.where(holder == me, location, jnp.where(holder < me, up_at, count + dn_at))
    scalars = (first, last, low, high, source, place)

    full = lax.all_gather(tokens, "tp", axis=1, tiled=True)

    sizes = [k for k in (6, 7, 8, 9, 10) if k < count] + [count]

    def branch(number, slots):
        def run(up_location, dn_location, flags):
            packed = pack(jnp.concatenate([up_location[:slots], dn_location[:slots]]), down_f, up_q, up_v)
            return sweep(n, slots, count, number + 1, flags, packed)

        return run

    pick = sum((most[0] > k).astype(jnp.int32) for k in sizes[:-1])
    swept = lax.switch(pick, [branch(i, k) for i, k in enumerate(sizes)], up_location, dn_location, flags)

    partial = down_products(scalars, tokens, swept, down_f)
    down = lax.psum(partial, "tp").astype(jnp.bfloat16)
    base_q = jnp.dot(full, query_weight, preferred_element_type=jnp.float32)
    base_v = jnp.dot(full, value_weight, preferred_element_type=jnp.float32)
    return tuple(up_products(scalars, down, base_q, base_v, swept, up_q, up_v))


def solution(mesh):
    in_specs = (
        P(("replica", "dp"), "tp"),
        P(None, "tp"),
        P(None, "tp"),
        P("dp", "tp", None),
        P("dp", None, "tp"),
        P("dp", None, "tp"),
        P("replica"),
        P("replica"),
        P(),
    )
    out_specs = (P(("replica", "dp"), "tp"), P(("replica", "dp"), "tp"))
    run = functools.partial(body, mesh.shape["replica"], mesh.shape["dp"])
    return jax.shard_map(run, mesh=mesh, in_specs=in_specs, out_specs=out_specs, check_vma=False)
```

```python
import functools

import jax
import jax.numpy as jnp
from jax import lax
from jax.experimental import pallas as pl
from jax.experimental.pallas import tpu as pltpu
from jax.sharding import PartitionSpec as P

adapter_scale = 0.5
LANES = 128
PARTS = 4
LAG = 3
ROWS = 128
MESH = pl.DeviceIdType.MESH
HBM = pl.BlockSpec(memory_space=pl.ANY)
SMEM = pl.BlockSpec(memory_space=pltpu.SMEM)
VMEM = pl.BlockSpec(memory_space=pltpu.VMEM)
GRANT = 60 << 20


def chunks_of(columns):
    return -(-columns // LANES)


def pack_kernel(keys, down_ref, up_q_ref, up_v_ref, out_ref):
    depth = down_ref.shape[1]
    rank = up_q_ref.shape[1]
    out_ref[0, pl.ds(0, depth), :] = down_ref[0]
    at = depth
    for ref in (up_q_ref, up_v_ref):
        columns = ref.shape[2]
        for j in range(chunks_of(columns)):
            width = min(LANES, columns - j * LANES)
            out_ref[0, pl.ds(at, rank), pl.ds(0, width)] = ref[0, :, pl.ds(j * LANES, width)]
            if width < LANES:
                out_ref[0, pl.ds(at, rank), pl.ds(width, LANES - width)] = jnp.zeros(
                    (rank, LANES - width), out_ref.dtype
                )
            at += rank


def pack(locations, down_f, up_q, up_v):
    count = locations.shape[0]
    depth, rank = down_f.shape[1], up_q.shape[1]
    height = depth + rank * (chunks_of(up_q.shape[2]) + chunks_of(up_v.shape[2]))
    return pl.pallas_call(
        pack_kernel,
        grid_spec=pltpu.PrefetchScalarGridSpec(
            num_scalar_prefetch=1,
            grid=(count,),
            in_specs=[
                pl.BlockSpec((1,) + t.shape[1:], lambda i, keys: (keys[i], 0, 0))
                for t in (down_f, up_q, up_v)
            ],
            out_specs=pl.BlockSpec((1, height, LANES), lambda i, keys: (i, 0, 0)),
        ),
        out_shape=jax.ShapeDtypeStruct((count, height, LANES), down_f.dtype),
        name="pack",
    )(locations, down_f, up_q, up_v)


def sweep_kernel(n, slots, spread, own_flag, packed, out, own, held, load_sem, send_sem, recv_sem, save_sem):
    me = lax.axis_index("dp")
    piece = held.shape[1] // PARTS
    steps = slots * PARTS
    barrier = pltpu.get_barrier_semaphore()
    has_low, has_high = me > 0, me < n - 1

    @pl.when(has_low)
    def _():
        pl.semaphore_signal(barrier, inc=1, device_id={"dp": me - 1}, device_id_type=MESH)

    @pl.when(has_high)
    def _():
        pl.semaphore_signal(barrier, inc=1, device_id={"dp": me + 1}, device_id_type=MESH)

    def load(i):
        return pltpu.make_async_copy(packed.at[i], own.at[i], load_sem.at[i])

    def start_load(i, carry):
        load(i).start()
        return carry

    lax.fori_loop(0, 2 * slots, start_load, 0)

    pl.semaphore_wait(barrier, has_low.astype(jnp.int32) + has_high.astype(jnp.int32))

    lower = me < n // 2

    def span(c):
        return lax.rem(c, PARTS) * piece

    def copy(stream, c, source, target):
        i = stream * slots + c // PARTS
        rows = pl.ds(span(c), piece)
        k = stream * steps + c
        return pltpu.make_async_remote_copy(
            src_ref=source.at[i, rows],
            dst_ref=held.at[i, rows],
            send_sem=send_sem.at[k],
            recv_sem=recv_sem.at[k],
            device_id={"dp": target},
            device_id_type=MESH,
        )

    def save(stream, c):
        i = stream * slots + c // PARTS
        rows = pl.ds(span(c), piece)
        return pltpu.make_async_copy(
            held.at[i, rows], out.at[stream * spread + c // PARTS, rows], save_sem.at[stream * steps + c]
        )

    def wait_load(i, carry):
        load(i).wait()
        return carry

    lax.fori_loop(0, 2 * slots, wait_load, 0)

    def first_sends(stream, target):
        def step(c, carry):
            copy(stream, c, own, target).start()
            return carry

        lax.fori_loop(0, steps, step, 0)

    @pl.when(jnp.logical_not(has_low))
    def _():
        first_sends(0, me + 1)

    @pl.when(jnp.logical_not(has_high))
    def _():
        first_sends(1, me - 1)

    def handle(stream, c):
        comes = has_low if stream == 0 else has_high
        goes = has_high if stream == 0 else has_low
        target = jnp.minimum(me + 1, n - 1) if stream == 0 else jnp.maximum(me - 1, 0)

        @pl.when(comes)
        def _():
            copy(stream, c, own, target).wait_recv()
            i = stream * slots + c // PARTS
            rows = pl.ds(pl.multiple_of(span(c), 16), piece)
            flag = own_flag[stream * spread + c // PARTS]
            save(stream, c).start()

            @pl.when(goes)
            def _():
                own[i, rows, :] = jnp.where(flag > 0, own[i, rows, :], held[i, rows, :])
                copy(stream, c, own, target).start()


    def step(t, carry):
        late = t - LAG

        @pl.when(jnp.logical_and(lower, t < steps))
        def _():
            handle(0, t)

        @pl.when(jnp.logical_and(lower, late >= 0))
        def _():
            handle(1, late)

        @pl.when(jnp.logical_and(jnp.logical_not(lower), t < steps))
        def _():
            handle(1, t)

        @pl.when(jnp.logical_and(jnp.logical_not(lower), late >= 0))
        def _():
            handle(0, late)

        return carry

    lax.fori_loop(0, steps + LAG, step, 0)

    def finish(c, carry):
        @pl.when(has_high)
        def _():
            copy(0, c, own, jnp.minimum(me + 1, n - 1)).wait_send()

        @pl.when(has_low)
        def _():
            copy(1, c, own, jnp.maximum(me - 1, 0)).wait_send()
            save(0, c).wait()

        @pl.when(has_high)
        def _():
            save(1, c).wait()

        return carry

    lax.fori_loop(0, steps, finish, 0)


def sweep(n, slots, spread, number, own_flag, packed):
    height = packed.shape[1]
    steps = slots * PARTS
    return pl.pallas_call(
        functools.partial(sweep_kernel, n, slots, spread),
        out_shape=jax.ShapeDtypeStruct((2 * spread, height, LANES), packed.dtype),
        in_specs=[SMEM, HBM],
        out_specs=HBM,
        scratch_shapes=[
            pltpu.VMEM((2 * slots, height, LANES), packed.dtype),
            pltpu.VMEM((2 * slots, height, LANES), packed.dtype),
            pltpu.SemaphoreType.DMA((2 * slots,)),
            pltpu.SemaphoreType.DMA((2 * steps,)),
            pltpu.SemaphoreType.DMA((2 * steps,)),
            pltpu.SemaphoreType.DMA((2 * steps,)),
        ],
        compiler_params=pltpu.CompilerParams(
            collective_id=number, has_side_effects=True, vmem_limit_bytes=GRANT
        ),
        name="sweep%d" % slots,
    )(own_flag, packed)


def down_kernel(first, last, low, high, source, place, tokens, swept, store, out, factor, sem):
    depth = factor.shape[1]

    def fetch(r, act):
        slot = lax.rem(r, 2)

        @pl.when(source[r] == 0)
        def _():
            act(pltpu.make_async_copy(store.at[place[r]], factor.at[slot], sem.at[slot]))

        @pl.when(source[r] != 0)
        def _():
            act(pltpu.make_async_copy(swept.at[place[r], pl.ds(0, depth)], factor.at[slot], sem.at[slot]))

    fetch(first[0], lambda c: c.start())

    def request(r, carry):
        @pl.when(r + 1 < last[0])
        def _():
            fetch(r + 1, lambda c: c.start())

        fetch(r, lambda c: c.wait())
        slot = lax.rem(r, 2)

        def block(k, inner):
            rows = pl.ds(pl.multiple_of(k * ROWS, ROWS), ROWS)
            product = jnp.dot(tokens[rows, :], factor[slot], preferred_element_type=jnp.float32)
            at = k * ROWS + lax.broadcasted_iota(jnp.int32, product.shape, 0)
            inside = jnp.logical_and(at >= low[r], at < high[r])
            out[rows, :] = jnp.where(inside, product, out[rows, :])
            return inner

        lax.fori_loop(low[r] // ROWS, (high[r] + ROWS - 1) // ROWS, block, 0)
        return carry

    lax.fori_loop(first[0], last[0], request, 0)


def down_products(scalars, tokens, swept, store):
    return pl.pallas_call(
        down_kernel,
        out_shape=jax.ShapeDtypeStruct((tokens.shape[0], store.shape[2]), jnp.float32),
        in_specs=[SMEM] * 6 + [VMEM, HBM, HBM],
        out_specs=VMEM,
        scratch_shapes=[
            pltpu.VMEM((2,) + store.shape[1:], store.dtype),
            pltpu.SemaphoreType.DMA((2,)),
        ],
        compiler_params=pltpu.CompilerParams(vmem_limit_bytes=24 << 20),
        name="down",
    )(*scalars, tokens, swept, store)


def up_kernel(
    first, last, low, high, source, place, down, base_q, base_v, swept, up_q, up_v,
    out_q, out_v, low_q, low_v, strip, own_q, own_v, sem,
):
    rank = own_q.shape[1]
    depth = swept.shape[1] - strip.shape[1]

    def fetch(r, act):
        slot = lax.rem(r, 2)

        @pl.when(source[r] == 0)
        def _():
            act(pltpu.make_async_copy(up_q.at[place[r]], own_q.at[slot], sem.at[slot, 0]))
            act(pltpu.make_async_copy(up_v.at[place[r]], own_v.at[slot], sem.at[slot, 1]))

        @pl.when(source[r] != 0)
        def _():
            act(pltpu.make_async_copy(
                swept.at[place[r], pl.ds(depth, strip.shape[1])], strip.at[slot], sem.at[slot, 0]))

    fetch(first[0], lambda c: c.start())

    def request(r, carry):
        @pl.when(r + 1 < last[0])
        def _():
            fetch(r + 1, lambda c: c.start())

        fetch(r, lambda c: c.wait())
        slot = lax.rem(r, 2)

        @pl.when(source[r] != 0)
        def _():
            at = 0
            for ref in (own_q, own_v):
                columns = ref.shape[2]
                for j in range(chunks_of(columns)):
                    width = min(LANES, columns - j * LANES)
                    ref[slot, :, pl.ds(j * LANES, width)] = strip[slot, pl.ds(at, rank), pl.ds(0, width)]
                    at += rank

        def block(k, inner):
            rows = pl.ds(pl.multiple_of(k * ROWS, ROWS), ROWS)
            at = k * ROWS + lax.broadcasted_iota(jnp.int32, (ROWS, 1), 0)
            inside = jnp.logical_and(at >= low[r], at < high[r])
            half = down[rows, :]
            for mine, factor, total in ((half[:, :rank], own_q, low_q), (half[:, rank:], own_v, low_v)):
                product = jnp.dot(mine, factor[slot], preferred_element_type=jnp.float32)
                total[rows, :] = jnp.where(inside, product, total[rows, :])
            return inner

        lax.fori_loop(low[r] // ROWS, (high[r] + ROWS - 1) // ROWS, block, 0)
        return carry

    lax.fori_loop(first[0], last[0], request, 0)

    def close(k, carry):
        rows = pl.ds(pl.multiple_of(k * ROWS, ROWS), ROWS)
        out_q[rows, :] = (base_q[rows, :] + adapter_scale * low_q[rows, :]).astype(out_q.dtype)
        out_v[rows, :] = (base_v[rows, :] + adapter_scale * low_v[rows, :]).astype(out_v.dtype)
        return carry

    lax.fori_loop(0, down.shape[0] // ROWS, close, 0)


def up_products(scalars, down, base_q, base_v, swept, up_q, up_v):
    strip = up_q.shape[1] * (chunks_of(up_q.shape[2]) + chunks_of(up_v.shape[2]))
    return pl.pallas_call(
        up_kernel,
        out_shape=[jax.ShapeDtypeStruct(b.shape, jnp.bfloat16) for b in (base_q, base_v)],
        in_specs=[SMEM] * 6 + [VMEM] * 3 + [HBM] * 3,
        out_specs=[VMEM, VMEM],
        scratch_shapes=[
            pltpu.VMEM(base_q.shape, jnp.float32),
            pltpu.VMEM(base_v.shape, jnp.float32),
            pltpu.VMEM((2, strip, LANES), swept.dtype),
            pltpu.VMEM((2,) + up_q.shape[1:], up_q.dtype),
            pltpu.VMEM((2,) + up_v.shape[1:], up_v.dtype),
            pltpu.SemaphoreType.DMA((2, 2)),
        ],
        compiler_params=pltpu.CompilerParams(vmem_limit_bytes=40 << 20),
        name="up",
    )(*scalars, down, base_q, base_v, swept, up_q, up_v)


def travel(n, me, begins, ends, slot, location):
    count = slot.shape[0]
    index = jnp.arange(count, dtype=jnp.int32)
    goes = ends > begins
    same = (slot[:, None] == slot[None, :])[None] & goes[:, None, :]
    first = jnp.min(jnp.where(same, index, count), axis=2)
    leads = goes & (first == index)
    reach = jnp.max(jnp.where(same, ends[:, None, :], -1), axis=2)
    link = jnp.arange(n - 1, dtype=jnp.int32)[None, :, None]
    crosses = leads[:, None, :] & (begins[:, None, :] <= link) & (reach[:, None, :] > link)
    need = jnp.max(jnp.sum(crosses.astype(jnp.int32), axis=2))
    before = index[None, :] < index[:, None]
    lane = jnp.full(goes.shape, -1, jnp.int32)
    for node in range(n - 1):
        active = leads & (begins < node) & (reach > node)
        free = ~jnp.any(active[:, None, :] & (lane[:, None, :] == index[None, :, None]), axis=2)
        fresh = leads & (begins == node)
        order = jnp.sum((before[None] & fresh[:, None, :]).astype(jnp.int32), axis=2)
        free_order = jnp.sum((before[None] & free[:, None, :]).astype(jnp.int32), axis=2)
        chosen = free[:, None, :] & (free_order[:, None, :] == order[:, :, None])
        lane = jnp.where(fresh, jnp.sum(jnp.where(chosen, index, 0), axis=2), lane)
    starts_here = leads & (begins == me[:, None])
    put = starts_here[:, None, :] & (lane[:, None, :] == index[None, :, None])
    put_location = jnp.sum(jnp.where(put, location, 0), axis=2)
    put_flag = jnp.sum(put.astype(jnp.int32), axis=2)
    follows = index[None, None, :] == first[:, :, None]
    lane = jnp.sum(jnp.where(follows, lane[:, None, :], 0), axis=2)
    return need, lane, put_location, put_flag


def total_over(part, axis, size):
    if size & (size - 1):
        return lax.psum(part, axis)
    step = 1
    while step < size:
        part = part + lax.ppermute(part, axis, [(i, i ^ step) for i in range(size)])
        step *= 2
    return part


def body(replicas, width, n, tokens, query_weight, value_weight, down_f, up_q, up_v, request_adapter, lengths, home):
    tok_rows = tokens.shape[0]
    stored = down_f.shape[0]
    count = request_adapter.shape[0]
    me = lax.axis_index("dp")
    index = jnp.arange(count, dtype=jnp.int32)
    wide = jnp.arange(home.shape[0], dtype=jnp.int32)
    slot = jnp.sum(jnp.where(request_adapter[:, None] == wide[None, :], home[None, :], 0), axis=1)
    starts = jnp.sum(jnp.where(index[None, :] < index[:, None], lengths[None, :], 0), axis=1)
    ends = starts + lengths
    holder, location = slot // stored, slot % stored
    begin, end = starts // tok_rows, (ends - 1) // tok_rows
    need, lane, put_location, put_flag = travel(
        n,
        jnp.stack([me, n - 1 - me]),
        jnp.stack([holder, n - 1 - holder]),
        jnp.stack([end, n - 1 - begin]),
        slot,
        location,
    )
    need = need.reshape(1)
    most = need
    for shift in range(1, replicas):
        other = lax.ppermute(need, "replica", [(i, (i + shift) % replicas) for i in range(replicas)])
        most = jnp.maximum(most, other)
    flags = put_flag.reshape(-1)

    offset = me * tok_rows
    here = (begin <= me) & (end >= me)
    first = jnp.min(jnp.where(here, index, count)).reshape(1)
    last = jnp.max(jnp.where(here, index, -1)).reshape(1) + 1
    low = jnp.clip(starts - offset, 0, tok_rows)
    high = jnp.clip(ends - offset, 0, tok_rows)
    source = (holder != me).astype(jnp.int32)
    place = jnp.where(holder == me, location, jnp.where(holder < me, lane[0], count + lane[1]))
    scalars = (first, last, low, high, source, place)

    full = lax.all_gather(tokens, "tp", axis=1, tiled=True)

    sizes = [k for k in (3, 4, 5, 6, 7, 8, 10) if k < count] + [count]

    def branch(number, slots):
        def run(put_location, flags):
            packed = pack(put_location[:, :slots].reshape(-1), down_f, up_q, up_v)
            return sweep(n, slots, count, number + 1, flags, packed)

        return run

    pick = sum((most[0] > k).astype(jnp.int32) for k in sizes[:-1])
    swept = lax.switch(pick, [branch(i, k) for i, k in enumerate(sizes)], put_location, flags)

    partial = down_products(scalars, tokens, swept, down_f)
    partial, full = lax.optimization_barrier((partial, full))
    down = total_over(partial, "tp", width).astype(jnp.bfloat16)
    base_q = jnp.dot(full, query_weight, preferred_element_type=jnp.float32)
    base_v = jnp.dot(full, value_weight, preferred_element_type=jnp.float32)
    return tuple(up_products(scalars, down, base_q, base_v, swept, up_q, up_v))


def solution(mesh):
    in_specs = (
        P(("replica", "dp"), "tp"),
        P(None, "tp"),
        P(None, "tp"),
        P("dp", "tp", None),
        P("dp", None, "tp"),
        P("dp", None, "tp"),
        P("replica"),
        P("replica"),
        P(),
    )
    out_specs = (P(("replica", "dp"), "tp"), P(("replica", "dp"), "tp"))
    run = functools.partial(body, mesh.shape["replica"], mesh.shape["tp"], mesh.shape["dp"])
    return jax.shard_map(run, mesh=mesh, in_specs=in_specs, out_specs=out_specs, check_vma=False)
```

```python
import functools

import jax
import jax.numpy as jnp
from jax import lax
from jax.experimental import pallas as pl
from jax.experimental.pallas import tpu as pltpu
from jax.sharding import PartitionSpec as P

adapter_scale = 0.5
LANES = 128
LAG = 3
ROWS = 128
MESH = pl.DeviceIdType.MESH
HBM = pl.BlockSpec(memory_space=pl.ANY)
SMEM = pl.BlockSpec(memory_space=pltpu.SMEM)
VMEM = pl.BlockSpec(memory_space=pltpu.VMEM)
GRANT = 60 << 20


def chunks_of(columns):
    return -(-columns // LANES)


def parts_of(height, slots):
    most = 8 if slots <= 8 else 4
    return max(p for p in (1, 2, 4, 8) if p <= most and height % (16 * p) == 0)


def pack_kernel(keys, down_ref, up_q_ref, up_v_ref, out_ref):
    depth = down_ref.shape[1]
    rank = up_q_ref.shape[1]
    out_ref[0, pl.ds(0, depth), :] = down_ref[0]
    at = depth
    for ref in (up_q_ref, up_v_ref):
        columns = ref.shape[2]
        for j in range(chunks_of(columns)):
            width = min(LANES, columns - j * LANES)
            out_ref[0, pl.ds(at, rank), pl.ds(0, width)] = ref[0, :, pl.ds(j * LANES, width)]
            if width < LANES:
                out_ref[0, pl.ds(at, rank), pl.ds(width, LANES - width)] = jnp.zeros(
                    (rank, LANES - width), out_ref.dtype
                )
            at += rank


def pack(locations, down_f, up_q, up_v):
    count = locations.shape[0]
    depth, rank = down_f.shape[1], up_q.shape[1]
    height = depth + rank * (chunks_of(up_q.shape[2]) + chunks_of(up_v.shape[2]))
    return pl.pallas_call(
        pack_kernel,
        grid_spec=pltpu.PrefetchScalarGridSpec(
            num_scalar_prefetch=1,
            grid=(count,),
            in_specs=[
                pl.BlockSpec((1,) + t.shape[1:], lambda i, keys: (keys[i], 0, 0))
                for t in (down_f, up_q, up_v)
            ],
            out_specs=pl.BlockSpec((1, height, LANES), lambda i, keys: (i, 0, 0)),
        ),
        out_shape=jax.ShapeDtypeStruct((count, height, LANES), down_f.dtype),
        name="pack",
    )(locations, down_f, up_q, up_v)


def sweep_kernel(n, slots, spread, own_flag, packed, out, own, held, load_sem, send_sem, recv_sem, save_sem):
    me = lax.axis_index("dp")
    parts = parts_of(held.shape[1], slots)
    piece = held.shape[1] // parts
    steps = slots * parts
    barrier = pltpu.get_barrier_semaphore()
    has_low, has_high = me > 0, me < n - 1

    @pl.when(has_low)
    def _():
        pl.semaphore_signal(barrier, inc=1, device_id={"dp": me - 1}, device_id_type=MESH)

    @pl.when(has_high)
    def _():
        pl.semaphore_signal(barrier, inc=1, device_id={"dp": me + 1}, device_id_type=MESH)

    def load(i):
        return pltpu.make_async_copy(packed.at[i], own.at[i], load_sem.at[i])

    def start_load(i, carry):
        @pl.when(has_high)
        def _():
            load(i).start()

        @pl.when(has_low)
        def _():
            load(slots + i).start()

        return carry

    lax.fori_loop(0, slots, start_load, 0)

    pl.semaphore_wait(barrier, has_low.astype(jnp.int32) + has_high.astype(jnp.int32))

    lower = me < n // 2

    def span(c):
        return lax.rem(c, parts) * piece

    def copy(stream, c, source, target):
        i = stream * slots + c // parts
        rows = pl.ds(span(c), piece)
        k = stream * steps + c
        return pltpu.make_async_remote_copy(
            src_ref=source.at[i, rows],
            dst_ref=held.at[i, rows],
            send_sem=send_sem.at[k],
            recv_sem=recv_sem.at[k],
            device_id={"dp": target},
            device_id_type=MESH,
        )

    def save(stream, c):
        i = stream * slots + c // parts
        rows = pl.ds(span(c), piece)
        return pltpu.make_async_copy(
            held.at[i, rows], out.at[stream * spread + c // parts, rows], save_sem.at[stream * steps + c]
        )

    def wait_load(stream, c):
        @pl.when(lax.rem(c, parts) == 0)
        def _():
            load(stream * slots + c // parts).wait()

    def first_sends(stream, target):
        def step(c, carry):
            wait_load(stream, c)
            copy(stream, c, own, target).start()
            return carry

        lax.fori_loop(0, steps, step, 0)

    @pl.when(jnp.logical_not(has_low))
    def _():
        first_sends(0, me + 1)

    @pl.when(jnp.logical_not(has_high))
    def _():
        first_sends(1, me - 1)

    def handle(stream, c):
        comes = has_low if stream == 0 else has_high
        goes = has_high if stream == 0 else has_low
        target = jnp.minimum(me + 1, n - 1) if stream == 0 else jnp.maximum(me - 1, 0)

        @pl.when(comes)
        def _():
            copy(stream, c, own, target).wait_recv()
            i = stream * slots + c // parts
            rows = pl.ds(pl.multiple_of(span(c), 16), piece)
            flag = own_flag[stream * spread + c // parts]
            save(stream, c).start()

            @pl.when(goes)
            def _():
                wait_load(stream, c)
                own[i, rows, :] = jnp.where(flag > 0, own[i, rows, :], held[i, rows, :])
                copy(stream, c, own, target).start()


    def step(t, carry):
        late = t - LAG

        @pl.when(jnp.logical_and(lower, t < steps))
        def _():
            handle(0, t)

        @pl.when(jnp.logical_and(lower, late >= 0))
        def _():
            handle(1, late)

        @pl.when(jnp.logical_and(jnp.logical_not(lower), t < steps))
        def _():
            handle(1, t)

        @pl.when(jnp.logical_and(jnp.logical_not(lower), late >= 0))
        def _():
            handle(0, late)

        return carry

    lax.fori_loop(0, steps + LAG, step, 0)

    def finish(c, carry):
        @pl.when(has_high)
        def _():
            copy(0, c, own, jnp.minimum(me + 1, n - 1)).wait_send()

        @pl.when(has_low)
        def _():
            copy(1, c, own, jnp.maximum(me - 1, 0)).wait_send()
            save(0, c).wait()

        @pl.when(has_high)
        def _():
            save(1, c).wait()

        return carry

    lax.fori_loop(0, steps, finish, 0)


def sweep(n, slots, spread, number, own_flag, packed):
    height = packed.shape[1]
    steps = slots * parts_of(height, slots)
    return pl.pallas_call(
        functools.partial(sweep_kernel, n, slots, spread),
        out_shape=jax.ShapeDtypeStruct((2 * spread, height, LANES), packed.dtype),
        in_specs=[SMEM, HBM],
        out_specs=HBM,
        scratch_shapes=[
            pltpu.VMEM((2 * slots, height, LANES), packed.dtype),
            pltpu.VMEM((2 * slots, height, LANES), packed.dtype),
            pltpu.SemaphoreType.DMA((2 * slots,)),
            pltpu.SemaphoreType.DMA((2 * steps,)),
            pltpu.SemaphoreType.DMA((2 * steps,)),
            pltpu.SemaphoreType.DMA((2 * steps,)),
        ],
        compiler_params=pltpu.CompilerParams(
            collective_id=number, has_side_effects=True, vmem_limit_bytes=GRANT
        ),
        name="sweep%d" % slots,
    )(own_flag, packed)


def down_kernel(first, last, low, high, source, place, tokens, swept, store, out, factor, sem):
    depth = factor.shape[1]

    def fetch(r, act):
        slot = lax.rem(r, 2)

        @pl.when(source[r] == 0)
        def _():
            act(pltpu.make_async_copy(store.at[place[r]], factor.at[slot], sem.at[slot]))

        @pl.when(source[r] != 0)
        def _():
            act(pltpu.make_async_copy(swept.at[place[r], pl.ds(0, depth)], factor.at[slot], sem.at[slot]))

    fetch(first[0], lambda c: c.start())

    def request(r, carry):
        @pl.when(r + 1 < last[0])
        def _():
            fetch(r + 1, lambda c: c.start())

        fetch(r, lambda c: c.wait())
        slot = lax.rem(r, 2)

        def block(k, inner):
            rows = pl.ds(pl.multiple_of(k * ROWS, ROWS), ROWS)
            product = jnp.dot(tokens[rows, :], factor[slot], preferred_element_type=jnp.float32)
            at = k * ROWS + lax.broadcasted_iota(jnp.int32, product.shape, 0)
            inside = jnp.logical_and(at >= low[r], at < high[r])
            out[rows, :] = jnp.where(inside, product, out[rows, :])
            return inner

        lax.fori_loop(low[r] // ROWS, (high[r] + ROWS - 1) // ROWS, block, 0)
        return carry

    lax.fori_loop(first[0], last[0], request, 0)


def down_products(scalars, tokens, swept, store):
    return pl.pallas_call(
        down_kernel,
        out_shape=jax.ShapeDtypeStruct((tokens.shape[0], store.shape[2]), jnp.float32),
        in_specs=[SMEM] * 6 + [VMEM, HBM, HBM],
        out_specs=VMEM,
        scratch_shapes=[
            pltpu.VMEM((2,) + store.shape[1:], store.dtype),
            pltpu.SemaphoreType.DMA((2,)),
        ],
        compiler_params=pltpu.CompilerParams(vmem_limit_bytes=24 << 20),
        name="down",
    )(*scalars, tokens, swept, store)


def up_kernel(
    first, last, low, high, source, place, down, base_q, base_v, swept, up_q, up_v,
    out_q, out_v, low_q, low_v, strip, own_q, own_v, sem,
):
    rank = own_q.shape[1]
    depth = swept.shape[1] - strip.shape[1]

    def fetch(r, act):
        slot = lax.rem(r, 2)

        @pl.when(source[r] == 0)
        def _():
            act(pltpu.make_async_copy(up_q.at[place[r]], own_q.at[slot], sem.at[slot, 0]))
            act(pltpu.make_async_copy(up_v.at[place[r]], own_v.at[slot], sem.at[slot, 1]))

        @pl.when(source[r] != 0)
        def _():
            act(pltpu.make_async_copy(
                swept.at[place[r], pl.ds(depth, strip.shape[1])], strip.at[slot], sem.at[slot, 0]))

    fetch(first[0], lambda c: c.start())

    def request(r, carry):
        @pl.when(r + 1 < last[0])
        def _():
            fetch(r + 1, lambda c: c.start())

        fetch(r, lambda c: c.wait())
        slot = lax.rem(r, 2)

        @pl.when(source[r] != 0)
        def _():
            at = 0
            for ref in (own_q, own_v):
                columns = ref.shape[2]
                for j in range(chunks_of(columns)):
                    width = min(LANES, columns - j * LANES)
                    ref[slot, :, pl.ds(j * LANES, width)] = strip[slot, pl.ds(at, rank), pl.ds(0, width)]
                    at += rank

        def block(k, inner):
            rows = pl.ds(pl.multiple_of(k * ROWS, ROWS), ROWS)
            at = k * ROWS + lax.broadcasted_iota(jnp.int32, (ROWS, 1), 0)
            inside = jnp.logical_and(at >= low[r], at < high[r])
            half = down[rows, :]
            for mine, factor, total in ((half[:, :rank], own_q, low_q), (half[:, rank:], own_v, low_v)):
                product = jnp.dot(mine, factor[slot], preferred_element_type=jnp.float32)
                total[rows, :] = jnp.where(inside, product, total[rows, :])
            return inner

        lax.fori_loop(low[r] // ROWS, (high[r] + ROWS - 1) // ROWS, block, 0)
        return carry

    lax.fori_loop(first[0], last[0], request, 0)

    def close(k, carry):
        rows = pl.ds(pl.multiple_of(k * ROWS, ROWS), ROWS)
        out_q[rows, :] = (base_q[rows, :] + adapter_scale * low_q[rows, :]).astype(out_q.dtype)
        out_v[rows, :] = (base_v[rows, :] + adapter_scale * low_v[rows, :]).astype(out_v.dtype)
        return carry

    lax.fori_loop(0, down.shape[0] // ROWS, close, 0)


def up_products(scalars, down, base_q, base_v, swept, up_q, up_v):
    strip = up_q.shape[1] * (chunks_of(up_q.shape[2]) + chunks_of(up_v.shape[2]))
    return pl.pallas_call(
        up_kernel,
        out_shape=[jax.ShapeDtypeStruct(b.shape, jnp.bfloat16) for b in (base_q, base_v)],
        in_specs=[SMEM] * 6 + [VMEM] * 3 + [HBM] * 3,
        out_specs=[VMEM, VMEM],
        scratch_shapes=[
            pltpu.VMEM(base_q.shape, jnp.float32),
            pltpu.VMEM(base_v.shape, jnp.float32),
            pltpu.VMEM((2, strip, LANES), swept.dtype),
            pltpu.VMEM((2,) + up_q.shape[1:], up_q.dtype),
            pltpu.VMEM((2,) + up_v.shape[1:], up_v.dtype),
            pltpu.SemaphoreType.DMA((2, 2)),
        ],
        compiler_params=pltpu.CompilerParams(vmem_limit_bytes=40 << 20),
        name="up",
    )(*scalars, down, base_q, base_v, swept, up_q, up_v)


def travel(n, me, begins, ends, slot, location):
    count = slot.shape[0]
    index = jnp.arange(count, dtype=jnp.int32)
    goes = ends > begins
    same = (slot[:, None] == slot[None, :])[None] & goes[:, None, :]
    first = jnp.min(jnp.where(same, index, count), axis=2)
    leads = goes & (first == index)
    reach = jnp.max(jnp.where(same, ends[:, None, :], -1), axis=2)
    link = jnp.arange(n - 1, dtype=jnp.int32)[None, :, None]
    crosses = leads[:, None, :] & (begins[:, None, :] <= link) & (reach[:, None, :] > link)
    need = jnp.max(jnp.sum(crosses.astype(jnp.int32), axis=2))
    before = index[None, :] < index[:, None]
    lane = jnp.full(goes.shape, -1, jnp.int32)
    for node in range(n - 1):
        active = leads & (begins < node) & (reach > node)
        free = ~jnp.any(active[:, None, :] & (lane[:, None, :] == index[None, :, None]), axis=2)
        fresh = leads & (begins == node)
        order = jnp.sum((before[None] & fresh[:, None, :]).astype(jnp.int32), axis=2)
        free_order = jnp.sum((before[None] & free[:, None, :]).astype(jnp.int32), axis=2)
        chosen = free[:, None, :] & (free_order[:, None, :] == order[:, :, None])
        lane = jnp.where(fresh, jnp.sum(jnp.where(chosen, index, 0), axis=2), lane)
    starts_here = leads & (begins == me[:, None])
    put = starts_here[:, None, :] & (lane[:, None, :] == index[None, :, None])
    put_location = jnp.sum(jnp.where(put, location, 0), axis=2)
    put_flag = jnp.sum(put.astype(jnp.int32), axis=2)
    follows = index[None, None, :] == first[:, :, None]
    lane = jnp.sum(jnp.where(follows, lane[:, None, :], 0), axis=2)
    return need, lane, put_location, put_flag


def total_over(part, axis, size):
    if size & (size - 1):
        return lax.psum(part, axis)
    step = 1
    while step < size:
        part = part + lax.ppermute(part, axis, [(i, i ^ step) for i in range(size)])
        step *= 2
    return part


def body(replicas, width, n, tokens, query_weight, value_weight, down_f, up_q, up_v, request_adapter, lengths, home):
    tok_rows = tokens.shape[0]
    stored = down_f.shape[0]
    count = request_adapter.shape[0]
    me = lax.axis_index("dp")
    index = jnp.arange(count, dtype=jnp.int32)
    wide = jnp.arange(home.shape[0], dtype=jnp.int32)
    slot = jnp.sum(jnp.where(request_adapter[:, None] == wide[None, :], home[None, :], 0), axis=1)
    starts = jnp.sum(jnp.where(index[None, :] < index[:, None], lengths[None, :], 0), axis=1)
    ends = starts + lengths
    holder, location = slot // stored, slot % stored
    begin, end = starts // tok_rows, (ends - 1) // tok_rows
    need, lane, put_location, put_flag = travel(
        n,
        jnp.stack([me, n - 1 - me]),
        jnp.stack([holder, n - 1 - holder]),
        jnp.stack([end, n - 1 - begin]),
        slot,
        location,
    )
    need = need.reshape(1)
    most = need
    for shift in range(1, replicas):
        other = lax.ppermute(need, "replica", [(i, (i + shift) % replicas) for i in range(replicas)])
        most = jnp.maximum(most, other)
    flags = put_flag.reshape(-1)

    offset = me * tok_rows
    here = (begin <= me) & (end >= me)
    first = jnp.min(jnp.where(here, index, count)).reshape(1)
    last = jnp.max(jnp.where(here, index, -1)).reshape(1) + 1
    low = jnp.clip(starts - offset, 0, tok_rows)
    high = jnp.clip(ends - offset, 0, tok_rows)
    source = (holder != me).astype(jnp.int32)
    place = jnp.where(holder == me, location, jnp.where(holder < me, lane[0], count + lane[1]))
    scalars = (first, last, low, high, source, place)

    full = lax.all_gather(tokens, "tp", axis=1, tiled=True)

    sizes = [k for k in (4, 5, 6, 7, 8, 9, 10, 12) if k < count] + [count]

    def branch(number, slots):
        def run(put_location, flags):
            packed = pack(put_location[:, :slots].reshape(-1), down_f, up_q, up_v)
            return sweep(n, slots, count, number + 1, flags, packed)

        return run

    pick = sum((most[0] > k).astype(jnp.int32) for k in sizes[:-1])
    swept = lax.switch(pick, [branch(i, k) for i, k in enumerate(sizes)], put_location, flags)

    partial = down_products(scalars, tokens, swept, down_f)
    partial, full = lax.optimization_barrier((partial, full))
    down = total_over(partial, "tp", width).astype(jnp.bfloat16)
    base_q = jnp.dot(full, query_weight, preferred_element_type=jnp.float32)
    base_v = jnp.dot(full, value_weight, preferred_element_type=jnp.float32)
    return tuple(up_products(scalars, down, base_q, base_v, swept, up_q, up_v))


def solution(mesh):
    in_specs = (
        P(("replica", "dp"), "tp"),
        P(None, "tp"),
        P(None, "tp"),
        P("dp", "tp", None),
        P("dp", None, "tp"),
        P("dp", None, "tp"),
        P("replica"),
        P("replica"),
        P(),
    )
    out_specs = (P(("replica", "dp"), "tp"), P(("replica", "dp"), "tp"))
    run = functools.partial(body, mesh.shape["replica"], mesh.shape["tp"], mesh.shape["dp"])
    return jax.shard_map(run, mesh=mesh, in_specs=in_specs, out_specs=out_specs, check_vma=False)
```

```python
import functools

import jax
import jax.numpy as jnp
from jax import lax
from jax.experimental import pallas as pl
from jax.experimental.pallas import tpu as pltpu
from jax.sharding import PartitionSpec as P

adapter_scale = 0.5
LANES = 128
LAG = 3
ROWS = 128
MESH = pl.DeviceIdType.MESH
HBM = pl.BlockSpec(memory_space=pl.ANY)
SMEM = pl.BlockSpec(memory_space=pltpu.SMEM)
VMEM = pl.BlockSpec(memory_space=pltpu.VMEM)
GRANT = 60 << 20


def chunks_of(columns):
    return -(-columns // LANES)


def parts_of(height, slots):
    most = 8 if slots <= 8 else 4
    return max(p for p in (1, 2, 4, 8) if p <= most and height % (16 * p) == 0)


def pack_kernel(keys, down_ref, up_q_ref, up_v_ref, out_ref):
    depth = down_ref.shape[1]
    rank = up_q_ref.shape[1]
    out_ref[0, pl.ds(0, depth), :] = down_ref[0]
    at = depth
    for ref in (up_q_ref, up_v_ref):
        columns = ref.shape[2]
        for j in range(chunks_of(columns)):
            width = min(LANES, columns - j * LANES)
            out_ref[0, pl.ds(at, rank), pl.ds(0, width)] = ref[0, :, pl.ds(j * LANES, width)]
            if width < LANES:
                out_ref[0, pl.ds(at, rank), pl.ds(width, LANES - width)] = jnp.zeros(
                    (rank, LANES - width), out_ref.dtype
                )
            at += rank


def pack(locations, down_f, up_q, up_v):
    count = locations.shape[0]
    depth, rank = down_f.shape[1], up_q.shape[1]
    height = depth + rank * (chunks_of(up_q.shape[2]) + chunks_of(up_v.shape[2]))
    return pl.pallas_call(
        pack_kernel,
        grid_spec=pltpu.PrefetchScalarGridSpec(
            num_scalar_prefetch=1,
            grid=(count,),
            in_specs=[
                pl.BlockSpec((1,) + t.shape[1:], lambda i, keys: (keys[i], 0, 0))
                for t in (down_f, up_q, up_v)
            ],
            out_specs=pl.BlockSpec((1, height, LANES), lambda i, keys: (i, 0, 0)),
        ),
        out_shape=jax.ShapeDtypeStruct((count, height, LANES), down_f.dtype),
        name="pack",
    )(locations, down_f, up_q, up_v)


def sweep_kernel(n, slots, spread, own_flag, packed, out, own, held, load_sem, send_sem, recv_sem, save_sem):
    me = lax.axis_index("dp")
    parts = parts_of(held.shape[1], slots)
    piece = held.shape[1] // parts
    steps = slots * parts
    barrier = pltpu.get_barrier_semaphore()
    has_low, has_high = me > 0, me < n - 1

    @pl.when(has_low)
    def _():
        pl.semaphore_signal(barrier, inc=1, device_id={"dp": me - 1}, device_id_type=MESH)

    @pl.when(has_high)
    def _():
        pl.semaphore_signal(barrier, inc=1, device_id={"dp": me + 1}, device_id_type=MESH)

    def load(i):
        return pltpu.make_async_copy(packed.at[i], own.at[i], load_sem.at[i])

    def start_load(i, carry):
        @pl.when(has_high)
        def _():
            load(i).start()

        @pl.when(has_low)
        def _():
            load(slots + i).start()

        return carry

    lax.fori_loop(0, slots, start_load, 0)

    pl.semaphore_wait(barrier, has_low.astype(jnp.int32) + has_high.astype(jnp.int32))

    lower = me < n // 2

    def span(c):
        return lax.rem(c, parts) * piece

    def copy(stream, c, source, target):
        i = stream * slots + c // parts
        rows = pl.ds(span(c), piece)
        k = stream * steps + c
        return pltpu.make_async_remote_copy(
            src_ref=source.at[i, rows],
            dst_ref=held.at[i, rows],
            send_sem=send_sem.at[k],
            recv_sem=recv_sem.at[k],
            device_id={"dp": target},
            device_id_type=MESH,
        )

    def save(stream, c):
        i = stream * slots + c // parts
        rows = pl.ds(span(c), piece)
        return pltpu.make_async_copy(
            held.at[i, rows], out.at[stream * spread + c // parts, rows], save_sem.at[stream * steps + c]
        )

    def wait_load(stream, c):
        @pl.when(lax.rem(c, parts) == 0)
        def _():
            load(stream * slots + c // parts).wait()

    def first_sends(stream, target):
        def step(c, carry):
            wait_load(stream, c)
            copy(stream, c, own, target).start()
            return carry

        lax.fori_loop(0, steps, step, 0)

    @pl.when(jnp.logical_not(has_low))
    def _():
        first_sends(0, me + 1)

    @pl.when(jnp.logical_not(has_high))
    def _():
        first_sends(1, me - 1)

    def handle(stream, c):
        comes = has_low if stream == 0 else has_high
        goes = has_high if stream == 0 else has_low
        target = jnp.minimum(me + 1, n - 1) if stream == 0 else jnp.maximum(me - 1, 0)

        @pl.when(comes)
        def _():
            copy(stream, c, own, target).wait_recv()
            i = stream * slots + c // parts
            rows = pl.ds(pl.multiple_of(span(c), 16), piece)
            flag = own_flag[stream * spread + c // parts]
            save(stream, c).start()

            @pl.when(goes)
            def _():
                wait_load(stream, c)
                own[i, rows, :] = jnp.where(flag > 0, own[i, rows, :], held[i, rows, :])
                copy(stream, c, own, target).start()


    def step(t, carry):
        late = t - LAG

        @pl.when(jnp.logical_and(lower, t < steps))
        def _():
            handle(0, t)

        @pl.when(jnp.logical_and(lower, late >= 0))
        def _():
            handle(1, late)

        @pl.when(jnp.logical_and(jnp.logical_not(lower), t < steps))
        def _():
            handle(1, t)

        @pl.when(jnp.logical_and(jnp.logical_not(lower), late >= 0))
        def _():
            handle(0, late)

        return carry

    lax.fori_loop(0, steps + LAG, step, 0)

    def finish(c, carry):
        @pl.when(has_high)
        def _():
            copy(0, c, own, jnp.minimum(me + 1, n - 1)).wait_send()

        @pl.when(has_low)
        def _():
            copy(1, c, own, jnp.maximum(me - 1, 0)).wait_send()
            save(0, c).wait()

        @pl.when(has_high)
        def _():
            save(1, c).wait()

        return carry

    lax.fori_loop(0, steps, finish, 0)


def sweep(n, slots, spread, number, own_flag, packed):
    height = packed.shape[1]
    steps = slots * parts_of(height, slots)
    return pl.pallas_call(
        functools.partial(sweep_kernel, n, slots, spread),
        out_shape=jax.ShapeDtypeStruct((2 * spread, height, LANES), packed.dtype),
        in_specs=[SMEM, HBM],
        out_specs=HBM,
        scratch_shapes=[
            pltpu.VMEM((2 * slots, height, LANES), packed.dtype),
            pltpu.VMEM((2 * slots, height, LANES), packed.dtype),
            pltpu.SemaphoreType.DMA((2 * slots,)),
            pltpu.SemaphoreType.DMA((2 * steps,)),
            pltpu.SemaphoreType.DMA((2 * steps,)),
            pltpu.SemaphoreType.DMA((2 * steps,)),
        ],
        compiler_params=pltpu.CompilerParams(
            collective_id=number, has_side_effects=True, vmem_limit_bytes=GRANT
        ),
        name="sweep%d" % slots,
    )(own_flag, packed)


def down_kernel(first, last, low, high, source, place, tokens, swept, store, out, factor, sem):
    depth = factor.shape[1]

    def fetch(r, act):
        slot = lax.rem(r, 2)

        @pl.when(source[r] == 0)
        def _():
            act(pltpu.make_async_copy(store.at[place[r]], factor.at[slot], sem.at[slot]))

        @pl.when(source[r] != 0)
        def _():
            act(pltpu.make_async_copy(swept.at[place[r], pl.ds(0, depth)], factor.at[slot], sem.at[slot]))

    fetch(first[0], lambda c: c.start())

    def request(r, carry):
        @pl.when(r + 1 < last[0])
        def _():
            fetch(r + 1, lambda c: c.start())

        fetch(r, lambda c: c.wait())
        slot = lax.rem(r, 2)

        def block(k, inner):
            rows = pl.ds(pl.multiple_of(k * ROWS, ROWS), ROWS)
            product = jnp.dot(tokens[rows, :], factor[slot], preferred_element_type=jnp.float32)
            at = k * ROWS + lax.broadcasted_iota(jnp.int32, product.shape, 0)
            inside = jnp.logical_and(at >= low[r], at < high[r])
            out[rows, :] = jnp.where(inside, product, out[rows, :])
            return inner

        lax.fori_loop(low[r] // ROWS, (high[r] + ROWS - 1) // ROWS, block, 0)
        return carry

    lax.fori_loop(first[0], last[0], request, 0)


def down_products(scalars, tokens, swept, store):
    return pl.pallas_call(
        down_kernel,
        out_shape=jax.ShapeDtypeStruct((tokens.shape[0], store.shape[2]), jnp.float32),
        in_specs=[SMEM] * 6 + [VMEM, HBM, HBM],
        out_specs=VMEM,
        scratch_shapes=[
            pltpu.VMEM((2,) + store.shape[1:], store.dtype),
            pltpu.SemaphoreType.DMA((2,)),
        ],
        compiler_params=pltpu.CompilerParams(vmem_limit_bytes=24 << 20),
        name="down",
    )(*scalars, tokens, swept, store)


def up_kernel(
    first, last, low, high, source, place, down, base_q, base_v, swept, up_q, up_v,
    out_q, out_v, low_q, low_v, strip, own_q, own_v, sem,
):
    rank = own_q.shape[1]
    depth = swept.shape[1] - strip.shape[1]

    def fetch(r, act):
        slot = lax.rem(r, 2)

        @pl.when(source[r] == 0)
        def _():
            act(pltpu.make_async_copy(up_q.at[place[r]], own_q.at[slot], sem.at[slot, 0]))
            act(pltpu.make_async_copy(up_v.at[place[r]], own_v.at[slot], sem.at[slot, 1]))

        @pl.when(source[r] != 0)
        def _():
            act(pltpu.make_async_copy(
                swept.at[place[r], pl.ds(depth, strip.shape[1])], strip.at[slot], sem.at[slot, 0]))

    fetch(first[0], lambda c: c.start())

    def request(r, carry):
        @pl.when(r + 1 < last[0])
        def _():
            fetch(r + 1, lambda c: c.start())

        fetch(r, lambda c: c.wait())
        slot = lax.rem(r, 2)

        @pl.when(source[r] != 0)
        def _():
            at = 0
            for ref in (own_q, own_v):
                columns = ref.shape[2]
                for j in range(chunks_of(columns)):
                    width = min(LANES, columns - j * LANES)
                    ref[slot, :, pl.ds(j * LANES, width)] = strip[slot, pl.ds(at, rank), pl.ds(0, width)]
                    at += rank

        def block(k, inner):
            rows = pl.ds(pl.multiple_of(k * ROWS, ROWS), ROWS)
            at = k * ROWS + lax.broadcasted_iota(jnp.int32, (ROWS, 1), 0)
            inside = jnp.logical_and(at >= low[r], at < high[r])
            half = down[rows, :]
            for mine, factor, total in ((half[:, :rank], own_q, low_q), (half[:, rank:], own_v, low_v)):
                product = jnp.dot(mine, factor[slot], preferred_element_type=jnp.float32)
                total[rows, :] = jnp.where(inside, product, total[rows, :])
            return inner

        lax.fori_loop(low[r] // ROWS, (high[r] + ROWS - 1) // ROWS, block, 0)
        return carry

    lax.fori_loop(first[0], last[0], request, 0)

    def close(k, carry):
        rows = pl.ds(pl.multiple_of(k * ROWS, ROWS), ROWS)
        out_q[rows, :] = (base_q[rows, :] + adapter_scale * low_q[rows, :]).astype(out_q.dtype)
        out_v[rows, :] = (base_v[rows, :] + adapter_scale * low_v[rows, :]).astype(out_v.dtype)
        return carry

    lax.fori_loop(0, down.shape[0] // ROWS, close, 0)


def up_products(scalars, down, base_q, base_v, swept, up_q, up_v):
    strip = up_q.shape[1] * (chunks_of(up_q.shape[2]) + chunks_of(up_v.shape[2]))
    return pl.pallas_call(
        up_kernel,
        out_shape=[jax.ShapeDtypeStruct(b.shape, jnp.bfloat16) for b in (base_q, base_v)],
        in_specs=[SMEM] * 6 + [VMEM] * 3 + [HBM] * 3,
        out_specs=[VMEM, VMEM],
        scratch_shapes=[
            pltpu.VMEM(base_q.shape, jnp.float32),
            pltpu.VMEM(base_v.shape, jnp.float32),
            pltpu.VMEM((2, strip, LANES), swept.dtype),
            pltpu.VMEM((2,) + up_q.shape[1:], up_q.dtype),
            pltpu.VMEM((2,) + up_v.shape[1:], up_v.dtype),
            pltpu.SemaphoreType.DMA((2, 2)),
        ],
        compiler_params=pltpu.CompilerParams(vmem_limit_bytes=40 << 20),
        name="up",
    )(*scalars, down, base_q, base_v, swept, up_q, up_v)


def travel(n, me, begins, ends, slot, location):
    count = slot.shape[0]
    index = jnp.arange(count, dtype=jnp.int32)
    goes = ends > begins
    same = (slot[:, None] == slot[None, :])[None] & goes[:, None, :]
    first = jnp.min(jnp.where(same, index, count), axis=2)
    leads = goes & (first == index)
    reach = jnp.max(jnp.where(same, ends[:, None, :], -1), axis=2)
    link = jnp.arange(n - 1, dtype=jnp.int32)[None, :, None]
    crosses = leads[:, None, :] & (begins[:, None, :] <= link) & (reach[:, None, :] > link)
    need = jnp.max(jnp.sum(crosses.astype(jnp.int32), axis=2))
    before = index[None, :] < index[:, None]
    lane = jnp.full(goes.shape, -1, jnp.int32)
    for node in range(n - 1):
        active = leads & (begins < node) & (reach > node)
        free = ~jnp.any(active[:, None, :] & (lane[:, None, :] == index[None, :, None]), axis=2)
        fresh = leads & (begins == node)
        order = jnp.sum((before[None] & fresh[:, None, :]).astype(jnp.int32), axis=2)
        free_order = jnp.sum((before[None] & free[:, None, :]).astype(jnp.int32), axis=2)
        chosen = free[:, None, :] & (free_order[:, None, :] == order[:, :, None])
        lane = jnp.where(fresh, jnp.sum(jnp.where(chosen, index, 0), axis=2), lane)
    starts_here = leads & (begins == me[:, None])
    put = starts_here[:, None, :] & (lane[:, None, :] == index[None, :, None])
    put_location = jnp.sum(jnp.where(put, location, 0), axis=2)
    put_flag = jnp.sum(put.astype(jnp.int32), axis=2)
    follows = index[None, None, :] == first[:, :, None]
    lane = jnp.sum(jnp.where(follows, lane[:, None, :], 0), axis=2)
    return need, lane, put_location, put_flag


def total_over(part, axis, size, beside):
    if size & (size - 1):
        return lax.psum(part, axis), beside
    step = 1
    while step < size:
        part = part + lax.ppermute(part, axis, [(i, i ^ step) for i in range(size)])
        if step == 1:
            part, beside = lax.optimization_barrier((part, beside))
        step *= 2
    return part, beside


def body(replicas, width, n, tokens, query_weight, value_weight, down_f, up_q, up_v, request_adapter, lengths, home):
    tok_rows = tokens.shape[0]
    stored = down_f.shape[0]
    count = request_adapter.shape[0]
    me = lax.axis_index("dp")
    index = jnp.arange(count, dtype=jnp.int32)
    wide = jnp.arange(home.shape[0], dtype=jnp.int32)
    slot = jnp.sum(jnp.where(request_adapter[:, None] == wide[None, :], home[None, :], 0), axis=1)
    starts = jnp.sum(jnp.where(index[None, :] < index[:, None], lengths[None, :], 0), axis=1)
    ends = starts + lengths
    holder, location = slot // stored, slot % stored
    begin, end = starts // tok_rows, (ends - 1) // tok_rows
    need, lane, put_location, put_flag = travel(
        n,
        jnp.stack([me, n - 1 - me]),
        jnp.stack([holder, n - 1 - holder]),
        jnp.stack([end, n - 1 - begin]),
        slot,
        location,
    )
    need = need.reshape(1)
    most = need
    for shift in range(1, replicas):
        other = lax.ppermute(need, "replica", [(i, (i + shift) % replicas) for i in range(replicas)])
        most = jnp.maximum(most, other)
    flags = put_flag.reshape(-1)

    offset = me * tok_rows
    here = (begin <= me) & (end >= me)
    first = jnp.min(jnp.where(here, index, count)).reshape(1)
    last = jnp.max(jnp.where(here, index, -1)).reshape(1) + 1
    low = jnp.clip(starts - offset, 0, tok_rows)
    high = jnp.clip(ends - offset, 0, tok_rows)
    source = (holder != me).astype(jnp.int32)
    place = jnp.where(holder == me, location, jnp.where(holder < me, lane[0], count + lane[1]))
    scalars = (first, last, low, high, source, place)

    full = lax.all_gather(tokens, "tp", axis=1, tiled=True)

    sizes = [k for k in (4, 5, 6, 7, 8, 9, 10, 12) if k < count] + [count]

    def branch(number, slots):
        def run(put_location, flags):
            packed = pack(put_location[:, :slots].reshape(-1), down_f, up_q, up_v)
            return sweep(n, slots, count, number + 1, flags, packed)

        return run

    pick = sum((most[0] > k).astype(jnp.int32) for k in sizes[:-1])
    swept = lax.switch(pick, [branch(i, k) for i, k in enumerate(sizes)], put_location, flags)

    partial = down_products(scalars, tokens, swept, down_f)
    partial, full = lax.optimization_barrier((partial, full))
    base_v = jnp.dot(full, value_weight, preferred_element_type=jnp.float32)
    total, base_v = total_over(partial, "tp", width, base_v)
    down = total.astype(jnp.bfloat16)
    base_q = jnp.dot(full, query_weight, preferred_element_type=jnp.float32)
    return tuple(up_products(scalars, down, base_q, base_v, swept, up_q, up_v))


def solution(mesh):
    in_specs = (
        P(("replica", "dp"), "tp"),
        P(None, "tp"),
        P(None, "tp"),
        P("dp", "tp", None),
        P("dp", None, "tp"),
        P("dp", None, "tp"),
        P("replica"),
        P("replica"),
        P(),
    )
    out_specs = (P(("replica", "dp"), "tp"), P(("replica", "dp"), "tp"))
    run = functools.partial(body, mesh.shape["replica"], mesh.shape["tp"], mesh.shape["dp"])
    return jax.shard_map(run, mesh=mesh, in_specs=in_specs, out_specs=out_specs, check_vma=False)
```
